32 devices in a mesh: fsdp: 8 (over z, y), ctx: 2 (over x), tensor: 2 (over core).
Axes of the slice: x: 2, y: 2, z: 4, core: 2. Of those that a mesh axis runs over, the one named last changes fastest.
Arguments:
- block_input: bfloat16 [8, 1024, 1024], P('fsdp', 'ctx'), may hold values from -6 to 6
- operator_gain: bfloat16 [1024], P('fsdp'), may hold values from 0.5 to 1.5
- query_weight: bfloat16 [1024, 1024], P('fsdp', 'tensor'), may hold values from -0.1875 to 0.1875
- key_weight: bfloat16 [1024, 512], P('fsdp', 'tensor'), may hold values from -0.1875 to 0.1875
- value_weight: bfloat16 [1024, 512], P('fsdp', 'tensor'), may hold values from -0.1875 to 0.1875
- output_weight: bfloat16 [1024, 1024], P('tensor', 'fsdp'), may hold values from -0.75 to 0.75
- feedforward_gain: bfloat16 [1024], P('fsdp'), may hold values from 0.5 to 1.5
- gate_weight: bfloat16 [1024, 4608], P('fsdp', 'tensor'), may hold values from -0.1875 to 0.1875
- up_weight: bfloat16 [1024, 4608], P('fsdp', 'tensor'), may hold values from -0.1875 to 0.1875
- down_weight: bfloat16 [4608, 1024], P('tensor', 'fsdp'), may hold values from -0.09375 to 0.09375
- query_gain: bfloat16 [64], P('fsdp'), may hold values from 0.6 to 4
- key_gain: bfloat16 [64], P('fsdp'), may hold values from 0.6 to 4
- cotangent: bfloat16 [8, 1024, 1024], P('fsdp', 'ctx'), may hold values from -6 to 6
Outputs:
- block_output: bfloat16 [8, 1024, 1024], P('fsdp', 'ctx')
- input_grad: float32 [8, 1024, 1024], P('fsdp', 'ctx')
- operator_gain_grad: float32 [1024], P('fsdp')
- query_weight_grad: float32 [1024, 1024], P('fsdp', 'tensor')
- key_weight_grad: float32 [1024, 512], P('fsdp', 'tensor')
- value_weight_grad: float32 [1024, 512], P('fsdp', 'tensor')
- output_weight_grad: float32 [1024, 1024], P('tensor', 'fsdp')
- feedforward_gain_grad: float32 [1024], P('fsdp')
- gate_weight_grad: float32 [1024, 4608], P('fsdp', 'tensor')
- up_weight_grad: float32 [1024, 4608], P('fsdp', 'tensor')
- down_weight_grad: float32 [4608, 1024], P('tensor', 'fsdp')
- query_gain_grad: float32 [64], P('fsdp')
- key_gain_grad: float32 [64], P('fsdp')
The draws below stay inside these ranges and needn't reach their ends.
All inputs are finite; a program needn't handle non-finite values.
Results may differ from the reference program's by a relative error of at most 0.024.
The reference program's roundings to bfloat16 on the way (of `normed_input`, `attended`, `normed_hidden`, `activation`, `attended_grad` and `score_grad`) count: a program that leaves them out, or rounds other values in their place, can miss the bound.
Values may be sent and summed in bfloat16 or wider, within the bound.
A program may use at most 192 MiB of HBM per device.

```python
import jax
import jax.numpy as jnp
from jax import lax

D = 1024
H = 16
KV = 8
HD = 64
FF = 4608
LEN = 1024
SEQS = 8


def draw_query_gain(key, part):
    base = jax.random.uniform(jax.random.fold_in(key, 11), (HD,), jnp.float32, 0.6, 1.6)
    return base.astype(jnp.bfloat16)


def draw_key_gain(key, part):
    base = jax.random.uniform(jax.random.fold_in(key, 13), (HD,), jnp.float32, 0.6, 1.6)
    return base.astype(jnp.bfloat16)


def shard_levels(stream_key, extent, shards, least, largest):
    def one(axis_at, parts):
        steps = jax.random.uniform(jax.random.fold_in(jax.random.fold_in(stream_key, 6), axis_at), (parts,), jnp.float32, least / len(shards), largest / len(shards))
        return jnp.repeat(jnp.exp(steps), extent[axis_at] // parts).reshape((-1,) + (1,) * (len(extent) - axis_at - 1))

    loudness = one(*shards[0])
    for cut in shards[1:]:
        loudness = loudness * one(*cut)
    return loudness


def normal_values(own_key, extent, scale, bound, shards=(), held_as=jnp.bfloat16):
    values = jax.random.normal(own_key, extent, jnp.float32) * scale
    if len(shards) > 0:
        values = shard_levels(own_key, extent, shards, -0.22, 0.18) * values
    return jnp.clip(values, min=-bound, max=bound).astype(held_as)


def setup_inputs(seed: int = 0) -> dict:
    arg_keys = jax.random.split(jax.random.key(seed), 14)
    block_input = normal_values(arg_keys[0], (SEQS, LEN, D), 1.0, 6.0, ((0, 8), (1, 2)))
    operator_gain = jnp.clip(1.0 + 0.1 * jax.random.normal(arg_keys[1], (D,), jnp.float32), 0.5, 1.5).astype(jnp.bfloat16)
    query_weight = normal_values(arg_keys[2], (D, H * HD), D ** -0.5, 0.1875, ((0, 8), (1, 2)))
    key_weight = normal_values(arg_keys[3], (D, KV * HD), D ** -0.5, 0.1875, ((0, 8), (1, 2)))
    value_weight = normal_values(arg_keys[4], (D, KV * HD), D ** -0.5, 0.1875, ((0, 8), (1, 2)))
    output_weight = normal_values(arg_keys[5], (H * HD, D), (H * HD // 16) ** -0.5, 0.75, ((0, 2), (1, 8)))
    feedforward_gain = jnp.clip(1.0 + 0.1 * jax.random.normal(arg_keys[6], (D,), jnp.float32), 0.5, 1.5).astype(jnp.bfloat16)
    gate_weight = normal_values(arg_keys[7], (D, FF), D ** -0.5, 0.1875, ((0, 8), (1, 2)))
    up_weight = normal_values(arg_keys[8], (D, FF), D ** -0.5, 0.1875, ((0, 8), (1, 2)))
    down_weight = normal_values(arg_keys[9], (FF, D), FF ** -0.5, 0.09375, ((0, 2), (1, 8)))
    query_gain = draw_query_gain(jax.random.fold_in(arg_keys[13], 71), 0)
    key_gain = draw_key_gain(jax.random.fold_in(arg_keys[13], 71), 0)
    cotangent = normal_values(arg_keys[12], (SEQS, LEN, D), 1.0, 6.0, ((0, 8), (1, 2)))
    return {"block_input": block_input, "operator_gain": operator_gain, "query_weight": query_weight, "key_weight": key_weight, "value_weight": value_weight, "output_weight": output_weight, "feedforward_gain": feedforward_gain, "gate_weight": gate_weight, "up_weight": up_weight, "down_weight": down_weight, "query_gain": query_gain, "key_gain": key_gain, "cotangent": cotangent}


EPS = 1e-05
THETA = 1000000.0

def rms_scale(values_in, gain):
    return values_in * lax.rsqrt(lax.optimization_barrier(jnp.mean(values_in * values_in, axis=-1, keepdims=True)) + EPS) * gain

def rotary_tables(positions, head_width):
    half_width = head_width // 2
    freqs = THETA ** (-jnp.arange(half_width).astype(jnp.float32) * 2.0 / head_width)
    angles = positions.astype(jnp.float32)[:, None] * freqs[None, :]
    return (jnp.cos(angles), jnp.sin(angles))

def rotate_halves(heads_in, cosine, sine):
    half_width = heads_in.shape[-1] // 2
    front_half = heads_in[..., :half_width]
    back_half = heads_in[..., half_width:]
    cos_rows = cosine[:, None, :]
    sin_rows = sine[:, None, :]
    return jnp.concatenate([front_half * cos_rows - back_half * sin_rows, back_half * cos_rows + front_half * sin_rows], axis=-1)

def head_prepare(raw, gain, cosine, sine):
    head_width = gain.shape[0]
    shaped = raw.reshape(raw.shape[:-1] + (raw.shape[-1] // head_width, head_width))
    return rotate_halves(rms_scale(shaped, gain), cosine, sine)

def swiglu(gate, upper):
    return jax.nn.silu(gate) * upper

def block_scores(query_block, keys, row_start):
    scale = queries_scale(query_block)
    scores = jnp.einsum('qhd,khd->hqk', query_block.astype(jnp.float32), keys.astype(jnp.float32)) * scale
    row_ids = row_start + jnp.arange(query_block.shape[0])
    col_ids = jnp.arange(keys.shape[0])
    allowed = col_ids[None, :] <= row_ids[:, None]
    return jnp.where(allowed[None, :, :], scores, -1e+30)

def queries_scale(query_block):
    return 1.0 / query_block.shape[-1] ** 0.5

def attend(queries, keys, values):
    length = queries.shape[0]
    block_rows = min(512, length)
    outputs = []
    totals = []
    for block_index in range(length // block_rows):
        start = block_index * block_rows
        scores = block_scores(queries[start:start + block_rows], keys, start)
        peak = lax.optimization_barrier(jnp.max(scores, axis=-1, keepdims=True))
        log_total = peak + jnp.log(lax.optimization_barrier(jnp.sum(jnp.exp(scores - peak), axis=-1, keepdims=True)))
        probs = jnp.exp(scores - log_total).astype(jnp.bfloat16)
        block_out = jnp.einsum('hqk,khd->qhd', probs.astype(jnp.float32), values.astype(jnp.float32))
        outputs.append(block_out.astype(jnp.bfloat16))
        totals.append(log_total[..., 0])
    return (jnp.concatenate(outputs, axis=0), jnp.concatenate(totals, axis=1))

def attend_grad(queries, keys, values, outputs, totals, out_grad):
    length = queries.shape[0]
    block_rows = min(512, length)
    scale = queries_scale(queries)
    key_acc = jnp.zeros(keys.shape, jnp.float32)
    value_acc = jnp.zeros(values.shape, jnp.float32)
    query_parts = []
    keys32 = keys.astype(jnp.float32)
    values32 = values.astype(jnp.float32)
    for block_index in range(length // block_rows):
        start = block_index * block_rows
        query_block = queries[start:start + block_rows]
        scores = block_scores(query_block, keys, start)
        probs = jnp.exp(scores - totals[:, start:start + block_rows][..., None])
        grad_block = out_grad[start:start + block_rows].astype(jnp.float32)
        value_acc = value_acc + jnp.einsum('hqk,qhd->khd', probs.astype(jnp.bfloat16).astype(jnp.float32), grad_block)
        prob_grad = jnp.einsum('qhd,khd->hqk', grad_block, values32)
        delta = lax.optimization_barrier(jnp.sum(grad_block * outputs[start:start + block_rows].astype(jnp.float32), axis=-1)).T
        score_grad = (probs * (prob_grad - delta[..., None])).astype(jnp.bfloat16).astype(jnp.float32)
        query_parts.append((jnp.einsum('hqk,khd->qhd', score_grad, keys32) * scale).astype(jnp.bfloat16))
        key_acc = key_acc + jnp.einsum('hqk,qhd->khd', score_grad, query_block.astype(jnp.float32)) * scale
    return (jnp.concatenate(query_parts, axis=0), key_acc.astype(jnp.bfloat16), value_acc.astype(jnp.bfloat16))

def reference(block_input, operator_gain, query_weight, key_weight, value_weight, output_weight, feedforward_gain, gate_weight, up_weight, down_weight, query_gain, key_gain, cotangent):
    head_width = query_gain.shape[0]
    group = H // KV
    length = block_input.shape[1]
    cosine, sine = rotary_tables(jnp.arange(length), head_width)
    operator_scale = operator_gain.astype(jnp.float32)
    feedforward_scale = feedforward_gain.astype(jnp.float32)
    query_scale = query_gain.astype(jnp.float32)
    key_scale = key_gain.astype(jnp.float32)

    def prepare(raw, gain):
        return head_prepare(raw, gain, cosine, sine)

    def one_sequence(carry, pair):
        tokens, upstream = pair
        input_flat = tokens.astype(jnp.float32)
        norm_one, norm_one_back = jax.vjp(rms_scale, input_flat, operator_scale)
        normed_input = norm_one.astype(jnp.bfloat16)
        query_raw = jnp.dot(normed_input, query_weight, preferred_element_type=jnp.float32)
        key_raw = jnp.dot(normed_input, key_weight, preferred_element_type=jnp.float32)
        value_raw = jnp.dot(normed_input, value_weight, preferred_element_type=jnp.float32)
        query_f32, query_back = jax.vjp(prepare, query_raw, query_scale)
        key_f32, key_back = jax.vjp(prepare, key_raw, key_scale)
        queries = query_f32.astype(jnp.bfloat16)
        keys = jnp.repeat(key_f32.astype(jnp.bfloat16), group, axis=1)
        values = jnp.repeat(value_raw.astype(jnp.bfloat16).reshape(length, KV, head_width), group, axis=1)
        head_out, head_total = attend(queries, keys, values)
        attended = head_out.reshape(length, H * head_width)
        hidden = input_flat + jnp.dot(attended, output_weight, preferred_element_type=jnp.float32)
        norm_two, norm_two_back = jax.vjp(rms_scale, hidden, feedforward_scale)
        normed_hidden = norm_two.astype(jnp.bfloat16)
        gate = jnp.dot(normed_hidden, gate_weight, preferred_element_type=jnp.float32)
        upper = jnp.dot(normed_hidden, up_weight, preferred_element_type=jnp.float32)
        act_f32, act_back = jax.vjp(swiglu, gate, upper)
        activation = act_f32.astype(jnp.bfloat16)
        output_f32 = hidden + jnp.dot(activation, down_weight, preferred_element_type=jnp.float32)
        block_output = output_f32.astype(jnp.bfloat16)
        down_grad = jnp.dot(activation.T, upstream, preferred_element_type=jnp.float32)
        act_grad = jnp.dot(upstream, down_weight.T, preferred_element_type=jnp.float32)
        gate_grad, upper_grad = act_back(act_grad)
        gate_grad = gate_grad.astype(jnp.bfloat16)
        upper_grad = upper_grad.astype(jnp.bfloat16)
        gate_weight_grad = jnp.dot(normed_hidden.T, gate_grad, preferred_element_type=jnp.float32)
        up_weight_grad = jnp.dot(normed_hidden.T, upper_grad, preferred_element_type=jnp.float32)
        normed_hidden_grad = jnp.dot(gate_grad, gate_weight.T, preferred_element_type=jnp.float32) + jnp.dot(upper_grad, up_weight.T, preferred_element_type=jnp.float32)
        hidden_norm_grad, feedforward_gain_grad = norm_two_back(normed_hidden_grad)
        hidden_grad = upstream.astype(jnp.float32) + hidden_norm_grad
        hidden_grad_b = hidden_grad.astype(jnp.bfloat16)
        output_weight_grad = jnp.dot(attended.T, hidden_grad_b, preferred_element_type=jnp.float32)
        attended_grad = jnp.dot(hidden_grad_b, output_weight.T, preferred_element_type=jnp.float32).astype(jnp.bfloat16).reshape(length, H, head_width)
        head_qgrad, head_kgrad, head_vgrad = attend_grad(queries, keys, values, head_out, head_total, attended_grad)
        key_sum = head_kgrad.astype(jnp.float32).reshape(length, KV, group, head_width).sum(axis=2)
        value_sum = head_vgrad.astype(jnp.float32).reshape(length, KV, group, head_width).sum(axis=2)
        query_pre, query_gain_grad = query_back(head_qgrad.astype(jnp.float32))
        key_pre, key_gain_grad = key_back(key_sum)
        query_raw_grad = query_pre.astype(jnp.bfloat16)
        key_raw_grad = key_pre.astype(jnp.bfloat16)
        value_raw_grad = value_sum.astype(jnp.bfloat16).reshape(length, KV * head_width)
        query_weight_grad = jnp.dot(normed_input.T, query_raw_grad, preferred_element_type=jnp.float32)
        key_weight_grad = jnp.dot(normed_input.T, key_raw_grad, preferred_element_type=jnp.float32)
        value_weight_grad = jnp.dot(normed_input.T, value_raw_grad, preferred_element_type=jnp.float32)
        normed_input_grad = jnp.dot(query_raw_grad, query_weight.T, preferred_element_type=jnp.float32) + jnp.dot(key_raw_grad, key_weight.T, preferred_element_type=jnp.float32) + jnp.dot(value_raw_grad, value_weight.T, preferred_element_type=jnp.float32)
        input_norm_grad, operator_gain_grad = norm_one_back(normed_input_grad)
        input_grad = hidden_grad + input_norm_grad
        grads = (operator_gain_grad, query_weight_grad, key_weight_grad, value_weight_grad, output_weight_grad, feedforward_gain_grad, gate_weight_grad, up_weight_grad, down_grad, query_gain_grad, key_gain_grad)
        carry = tuple((running + latest for running, latest in zip(carry, grads)))
        return (carry, (block_output, input_grad))
    initial = tuple((jnp.zeros(param.shape, jnp.float32) for param in (operator_gain, query_weight, key_weight, value_weight, output_weight, feedforward_gain, gate_weight, up_weight, down_weight, query_gain, key_gain)))
    totals, (outputs, input_grads) = lax.scan(one_sequence, initial, (block_input, cotangent))
    return (outputs, input_grads, totals[0], totals[1], totals[2], totals[3], totals[4], totals[5], totals[6], totals[7], totals[8], totals[9], totals[10])
```

```python
import jax
import jax.numpy as jnp
from jax import lax
from jax.sharding import PartitionSpec as P

EPS = 1e-05
THETA = 1000000.0


def rms_scale(values_in, gain):
    return (
        values_in * lax.rsqrt(jnp.mean(values_in * values_in, axis=-1, keepdims=True) + EPS) * gain
    )


def rotary_tables(positions, head_width):
    half_width = head_width // 2
    freqs = THETA ** (-jnp.arange(half_width).astype(jnp.float32) * 2.0 / head_width)
    angles = positions.astype(jnp.float32)[:, None] * freqs[None, :]
    return (jnp.cos(angles), jnp.sin(angles))


def rotate_halves(heads_in, cosine, sine):
    half_width = heads_in.shape[-1] // 2
    front_half = heads_in[..., :half_width]
    back_half = heads_in[..., half_width:]
    cos_rows = cosine[:, None, :]
    sin_rows = sine[:, None, :]
    return jnp.concatenate(
        [
            front_half * cos_rows - back_half * sin_rows,
            back_half * cos_rows + front_half * sin_rows,
        ],
        axis=-1,
    )


def head_prepare(raw, gain, cosine, sine):
    head_width = gain.shape[0]
    shaped = raw.reshape(raw.shape[:-1] + (raw.shape[-1] // head_width, head_width))
    return rotate_halves(rms_scale(shaped, gain), cosine, sine)


def swiglu(gate, upper):
    return jax.nn.silu(gate) * upper


def contract(left, right, left_dim, right_dim):
    return lax.dot_general(
        left, right, (((left_dim,), (right_dim,)), ((), ())), preferred_element_type=jnp.float32
    )


def block_scores(query_block, keys, query_pos, key_pos):
    scale = 1.0 / query_block.shape[-1] ** 0.5
    scores = (
        jnp.einsum("qhd,khd->hqk", query_block, keys, preferred_element_type=jnp.float32) * scale
    )
    allowed = key_pos[None, :] <= query_pos[:, None]
    return jnp.where(allowed[None, :, :], scores, -1e30)


def attend(queries, keys, values, positions):
    length = queries.shape[0]
    block_rows = min(512, length)
    outputs = []
    totals = []
    for start in range(0, length, block_rows):
        rows = slice(start, start + block_rows)
        scores = block_scores(queries[rows], keys, positions[rows], positions)
        peak = jnp.max(scores, axis=-1, keepdims=True)
        log_total = peak + jnp.log(jnp.sum(jnp.exp(scores - peak), axis=-1, keepdims=True))
        probs = jnp.exp(scores - log_total).astype(jnp.bfloat16)
        block_out = jnp.einsum("hqk,khd->qhd", probs, values, preferred_element_type=jnp.float32)
        outputs.append(block_out.astype(jnp.bfloat16))
        totals.append(log_total[..., 0])
    return (jnp.concatenate(outputs, axis=0), jnp.concatenate(totals, axis=1))


def attend_grad(queries, keys, values, outputs, totals, out_grad, positions):
    length = queries.shape[0]
    block_rows = min(512, length)
    scale = 1.0 / queries.shape[-1] ** 0.5
    key_acc = jnp.zeros(keys.shape, jnp.float32)
    value_acc = jnp.zeros(values.shape, jnp.float32)
    query_parts = []
    for start in range(0, length, block_rows):
        rows = slice(start, start + block_rows)
        query_block = queries[rows]
        scores = block_scores(query_block, keys, positions[rows], positions)
        probs = jnp.exp(scores - totals[:, rows][..., None])
        grad_block = out_grad[rows]
        value_acc = value_acc + jnp.einsum(
            "hqk,qhd->khd",
            probs.astype(jnp.bfloat16),
            grad_block,
            preferred_element_type=jnp.float32,
        )
        prob_grad = jnp.einsum(
            "qhd,khd->hqk", grad_block, values, preferred_element_type=jnp.float32
        )
        delta = jnp.sum(
            grad_block.astype(jnp.float32) * outputs[rows].astype(jnp.float32),
            axis=-1,
        ).T
        score_grad = (probs * (prob_grad - delta[..., None])).astype(jnp.bfloat16)
        query_parts.append(
            (
                jnp.einsum("hqk,khd->qhd", score_grad, keys, preferred_element_type=jnp.float32)
                * scale
            ).astype(jnp.bfloat16)
        )
        key_acc = (
            key_acc
            + jnp.einsum(
                "hqk,qhd->khd", score_grad, query_block, preferred_element_type=jnp.float32
            )
            * scale
        )
    return (
        jnp.concatenate(query_parts, axis=0),
        key_acc.astype(jnp.bfloat16),
        value_acc.astype(jnp.bfloat16),
    )


def shift(array, axis_name, step):
    size = lax.axis_size(axis_name)
    return lax.ppermute(array, axis_name, [(i, (i + step) % size) for i in range(size)])


def around(array, axis_name, dim):
    size = lax.axis_size(axis_name)
    return jnp.concatenate(
        [array] + [shift(array, axis_name, step) for step in range(1, size)], axis=dim
    )


def group_rows(array):
    return around(around(array, "ctx", 1), "tensor", 1)


def sum_around(array, axis_name):
    size = lax.axis_size(axis_name)
    part = array.shape[1] // size
    total = array[:, :part].astype(jnp.float32)
    for step in range(1, size):
        piece = array[:, step * part : (step + 1) * part].astype(jnp.bfloat16)
        total = total + shift(piece, axis_name, -step).astype(jnp.float32)
    return total


def group_sum(array):
    return sum_around(sum_around(array, "tensor"), "ctx")


def in_order(array, axis_name, dim):
    size = lax.axis_size(axis_name)
    me = lax.axis_index(axis_name)
    width = array.shape[dim]
    shape = list(array.shape)
    shape[dim] = width * size
    out = jnp.zeros(shape, array.dtype)
    for step in range(size):
        piece = array if step == 0 else shift(array, axis_name, step)
        owner = lax.rem(me - step + size, size)
        out = lax.dynamic_update_slice_in_dim(out, piece, owner * width, dim)
    return out


def part_of(array, dim, count, start):
    return lax.dynamic_slice_in_dim(array, start, count, dim)


def shards(
    block_input,
    operator_gain,
    query_weight,
    key_weight,
    value_weight,
    output_weight,
    feedforward_gain,
    gate_weight,
    up_weight,
    down_weight,
    query_gain,
    key_gain,
    cotangent,
):
    bf16 = jnp.bfloat16
    f32 = jnp.float32
    fsdp = lax.axis_size("fsdp")
    ctx = lax.axis_size("ctx")
    tensor = lax.axis_size("tensor")
    me_f = lax.axis_index("fsdp")
    me_c = lax.axis_index("ctx")
    me_t = lax.axis_index("tensor")
    seqs, tok_here, width = block_input.shape
    quarter = tok_here // tensor
    tokens = tok_here * ctx
    rows = seqs * tokens
    gain_rows = query_gain.shape[0]
    head_width = gain_rows * fsdp
    heads_shard = query_weight.shape[1] // head_width
    kv_shard = key_weight.shape[1] // head_width
    spread = heads_shard // kv_shard
    heads = heads_shard // ctx
    kv = max(1, kv_shard // ctx)
    group = heads // kv
    copies = max(1, ctx // kv_shard)
    q_cols = heads * head_width
    kv_cols = kv * head_width
    kv_start = ((me_c * heads) // spread) * head_width
    hidden_units = gate_weight.shape[1] // ctx
    shard_rows = query_weight.shape[0]

    gains = jnp.stack(
        [
            operator_gain,
            feedforward_gain,
            jnp.pad(query_gain, (0, shard_rows - gain_rows)),
            jnp.pad(key_gain, (0, shard_rows - gain_rows)),
        ],
        axis=1,
    )
    attention_pack = jnp.concatenate(
        [
            part_of(query_weight, 1, q_cols, me_c * q_cols),
            part_of(key_weight, 1, kv_cols, kv_start),
            part_of(value_weight, 1, kv_cols, kv_start),
            part_of(output_weight, 0, q_cols, me_c * q_cols).T,
            jnp.pad(gains, ((0, 0), (0, 124))),
        ],
        axis=1,
    )
    gate_up_pack = jnp.concatenate(
        [
            part_of(gate_weight, 1, hidden_units, me_c * hidden_units),
            part_of(up_weight, 1, hidden_units, me_c * hidden_units),
        ],
        axis=1,
    )
    down_pack = part_of(down_weight, 0, hidden_units, me_c * hidden_units).T
    attention_full = lax.all_gather(attention_pack, "fsdp", axis=0, tiled=True)
    gate_up_full = lax.all_gather(gate_up_pack, "fsdp", axis=0, tiled=True)
    down_full = lax.all_gather(down_pack, "fsdp", axis=0, tiled=True)
    qkv_cols = q_cols + 2 * kv_cols
    qkv_full = attention_full[:, :qkv_cols]
    output_full = attention_full[:, qkv_cols : qkv_cols + q_cols]
    gains_full = attention_full[:, qkv_cols + q_cols :].astype(f32)
    operator_scale = gains_full[:, 0]
    feedforward_scale = gains_full[:, 1]
    query_scale = gains_full[:, 2].reshape(fsdp, shard_rows)[:, :gain_rows].reshape(-1)
    key_scale = gains_full[:, 3].reshape(fsdp, shard_rows)[:, :gain_rows].reshape(-1)

    own_input = part_of(block_input, 1, quarter, me_t * quarter)
    all_input = group_rows(own_input).reshape(rows, width)
    upstream_own = part_of(cotangent, 1, quarter, me_t * quarter)
    upstream = group_rows(upstream_own).reshape(rows, width)

    ctx_order = lax.rem(me_c - jnp.arange(ctx) + ctx, ctx)
    tensor_order = lax.rem(me_t - jnp.arange(tensor) + tensor, tensor)
    positions = (
        tensor_order[:, None, None] * quarter
        + ctx_order[None, :, None] * tok_here
        + jnp.arange(quarter)[None, None, :]
    ).reshape(tokens)
    cosine, sine = rotary_tables(positions, head_width)

    def prepare(raw, gain):
        return head_prepare(raw, gain, cosine, sine)

    normed_input = rms_scale(all_input.astype(f32), operator_scale).astype(bf16)
    qkv_raw = jnp.dot(normed_input, qkv_full, preferred_element_type=f32).reshape(seqs, tokens, -1)
    query_f32, query_back = jax.vjp(prepare, qkv_raw[..., :q_cols], query_scale)
    key_f32, key_back = jax.vjp(prepare, qkv_raw[..., q_cols : q_cols + kv_cols], key_scale)
    queries = query_f32.astype(bf16)
    keys = jnp.repeat(key_f32.astype(bf16), group, axis=2)
    values = jnp.repeat(
        qkv_raw[..., q_cols + kv_cols :].astype(bf16).reshape(seqs, tokens, kv, head_width),
        group,
        axis=2,
    )
    attended, totals = jax.vmap(attend, in_axes=(0, 0, 0, None))(queries, keys, values, positions)
    attended_rows = attended.reshape(rows, q_cols)
    attention_part = contract(attended_rows, output_full, 1, 1).reshape(seqs, tokens, width)
    own_f32 = own_input.astype(f32)
    hidden = own_f32 + group_sum(attention_part)
    norm_two, norm_two_back = jax.vjp(rms_scale, hidden, feedforward_scale)
    normed_hidden = group_rows(norm_two.astype(bf16)).reshape(rows, width)
    gate_up = jnp.dot(normed_hidden, gate_up_full, preferred_element_type=f32)
    act_f32, act_back = jax.vjp(swiglu, gate_up[:, :hidden_units], gate_up[:, hidden_units:])
    activation = act_f32.astype(bf16)
    act_grad = jnp.dot(upstream, down_full, preferred_element_type=f32)
    gate_grad, up_grad = act_back(act_grad)
    gate_up_grad = jnp.concatenate([gate_grad.astype(bf16), up_grad.astype(bf16)], axis=1)
    hidden_part = contract(gate_up_grad, gate_up_full, 1, 1).reshape(seqs, tokens, width)
    normed_hidden_grad = group_sum(hidden_part)
    down_grad = contract(upstream, activation, 0, 0).astype(bf16)
    down_share = lax.psum_scatter(down_grad, "fsdp", scatter_dimension=0, tiled=True)
    gate_up_weight_grad = contract(normed_hidden, gate_up_grad, 0, 0).astype(bf16)
    gate_up_share = lax.psum_scatter(gate_up_weight_grad, "fsdp", scatter_dimension=0, tiled=True)
    down_part = contract(activation, down_full, 1, 1).reshape(seqs, tokens, width)
    own_output = (hidden + group_sum(down_part)).astype(bf16)
    block_output = in_order(own_output, "tensor", 1)

    hidden_norm_grad, feedforward_gain_grad = norm_two_back(normed_hidden_grad)
    hidden_grad = upstream_own.astype(f32) + hidden_norm_grad
    hidden_grad_b = group_rows(hidden_grad.astype(bf16)).reshape(rows, width)
    output_weight_grad = contract(hidden_grad_b, attended_rows, 0, 0)
    attended_grad = (
        jnp.dot(hidden_grad_b, output_full, preferred_element_type=f32)
        .astype(bf16)
        .reshape(seqs, tokens, heads, head_width)
    )
    query_hgrad, key_hgrad, value_hgrad = jax.vmap(attend_grad, in_axes=(0, 0, 0, 0, 0, 0, None))(
        queries, keys, values, attended, totals, attended_grad, positions
    )

    def head_sum(grad):
        return grad.astype(f32).reshape(seqs, tokens, kv, group, head_width).sum(axis=3)

    query_pre, query_gain_grad = query_back(query_hgrad.astype(f32))
    key_pre, key_gain_grad = key_back(head_sum(key_hgrad))
    qkv_raw_grad = jnp.concatenate(
        [
            query_pre.astype(bf16).reshape(rows, q_cols),
            key_pre.astype(bf16).reshape(rows, kv_cols),
            head_sum(value_hgrad).astype(bf16).reshape(rows, kv_cols),
        ],
        axis=1,
    )
    input_part = contract(qkv_raw_grad, qkv_full, 1, 1).reshape(seqs, tokens, width)
    normed_input_grad = group_sum(input_part)
    qkv_weight_grad = contract(normed_input, qkv_raw_grad, 0, 0)
    attention_grad = jnp.concatenate([qkv_weight_grad, output_weight_grad], axis=1).astype(bf16)
    attention_share = lax.psum_scatter(attention_grad, "fsdp", scatter_dimension=0, tiled=True)
    _, norm_one_back = jax.vjp(rms_scale, own_f32, operator_scale)
    input_norm_grad, operator_gain_grad = norm_one_back(normed_input_grad)
    input_grad = in_order(hidden_grad + input_norm_grad, "tensor", 1)

    gain_sums = lax.psum(
        jnp.concatenate([operator_gain_grad, feedforward_gain_grad, query_gain_grad, key_gain_grad]),
        ("fsdp", "ctx", "tensor"),
    )
    operator_share = part_of(gain_sums, 0, shard_rows, me_f * shard_rows)
    feedforward_share = part_of(gain_sums, 0, shard_rows, width + me_f * shard_rows)
    query_gain_share = part_of(gain_sums, 0, gain_rows, 2 * width + me_f * gain_rows)
    key_gain_share = part_of(gain_sums, 0, gain_rows, 2 * width + head_width + me_f * gain_rows)

    def spread_cols(share):
        return in_order(share, "ctx", 1).astype(f32)

    def spread_heads(share):
        if copies == 1:
            return spread_cols(share)
        every = in_order(share, "ctx", 1).astype(f32)
        return every.reshape(shard_rows, kv_shard, copies, head_width).sum(axis=2).reshape(
            shard_rows, -1
        )

    return (
        block_output,
        input_grad,
        operator_share,
        spread_cols(attention_share[:, :q_cols]),
        spread_heads(attention_share[:, q_cols : q_cols + kv_cols]),
        spread_heads(attention_share[:, q_cols + kv_cols : qkv_cols]),
        in_order(attention_share[:, qkv_cols:].T, "ctx", 0).astype(f32),
        feedforward_share,
        spread_cols(gate_up_share[:, :hidden_units]),
        spread_cols(gate_up_share[:, hidden_units:]),
        in_order(down_share.T, "ctx", 0).astype(f32),
        query_gain_share,
        key_gain_share,
    )


def solution(mesh):
    in_specs = (
        P("fsdp", "ctx", None),
        P("fsdp"),
        P("fsdp", "tensor"),
        P("fsdp", "tensor"),
        P("fsdp", "tensor"),
        P("tensor", "fsdp"),
        P("fsdp"),
        P("fsdp", "tensor"),
        P("fsdp", "tensor"),
        P("tensor", "fsdp"),
        P("fsdp"),
        P("fsdp"),
        P("fsdp", "ctx", None),
    )
    out_specs = (
        P("fsdp", "ctx", None),
        P("fsdp", "ctx", None),
        P("fsdp"),
        P("fsdp", "tensor"),
        P("fsdp", "tensor"),
        P("fsdp", "tensor"),
        P("tensor", "fsdp"),
        P("fsdp"),
        P("fsdp", "tensor"),
        P("fsdp", "tensor"),
        P("tensor", "fsdp"),
        P("fsdp"),
        P("fsdp"),
    )
    return jax.shard_map(shards, mesh=mesh, in_specs=in_specs, out_specs=out_specs, check_vma=False)
```

```python
import jax
import jax.numpy as jnp
from jax import lax
from jax.sharding import PartitionSpec as P

EPS = 1e-05
THETA = 1000000.0


def rms_scale(values_in, gain):
    return (
        values_in * lax.rsqrt(jnp.mean(values_in * values_in, axis=-1, keepdims=True) + EPS) * gain
    )


def rotary_tables(positions, head_width):
    half_width = head_width // 2
    freqs = THETA ** (-jnp.arange(half_width).astype(jnp.float32) * 2.0 / head_width)
    angles = positions.astype(jnp.float32)[:, None] * freqs[None, :]
    return (jnp.cos(angles), jnp.sin(angles))


def rotate_halves(heads_in, cosine, sine):
    half_width = heads_in.shape[-1] // 2
    front_half = heads_in[..., :half_width]
    back_half = heads_in[..., half_width:]
    cos_rows = cosine[:, None, :]
    sin_rows = sine[:, None, :]
    return jnp.concatenate(
        [
            front_half * cos_rows - back_half * sin_rows,
            back_half * cos_rows + front_half * sin_rows,
        ],
        axis=-1,
    )


def head_prepare(raw, gain, cosine, sine):
    head_width = gain.shape[0]
    shaped = raw.reshape(raw.shape[:-1] + (raw.shape[-1] // head_width, head_width))
    return rotate_halves(rms_scale(shaped, gain), cosine, sine)


def swiglu(gate, upper):
    return jax.nn.silu(gate) * upper


def contract(left, right, left_dim, right_dim):
    return lax.dot_general(
        left, right, (((left_dim,), (right_dim,)), ((), ())), preferred_element_type=jnp.float32
    )


def block_scores(query_block, keys, query_pos, key_pos):
    scale = 1.0 / query_block.shape[-1] ** 0.5
    scores = (
        jnp.einsum("qhd,khd->hqk", query_block, keys, preferred_element_type=jnp.float32) * scale
    )
    allowed = key_pos[None, :] <= query_pos[:, None]
    return jnp.where(allowed[None, :, :], scores, -1e30)


def attend(queries, keys, values, positions):
    length = queries.shape[0]
    block_rows = min(512, length)
    outputs = []
    totals = []
    for start in range(0, length, block_rows):
        rows = slice(start, start + block_rows)
        scores = block_scores(queries[rows], keys, positions[rows], positions)
        peak = jnp.max(scores, axis=-1, keepdims=True)
        log_total = peak + jnp.log(jnp.sum(jnp.exp(scores - peak), axis=-1, keepdims=True))
        probs = jnp.exp(scores - log_total).astype(jnp.bfloat16)
        block_out = jnp.einsum("hqk,khd->qhd", probs, values, preferred_element_type=jnp.float32)
        outputs.append(block_out.astype(jnp.bfloat16))
        totals.append(log_total[..., 0])
    return (jnp.concatenate(outputs, axis=0), jnp.concatenate(totals, axis=1))


def attend_grad(queries, keys, values, outputs, totals, out_grad, positions):
    length = queries.shape[0]
    block_rows = min(512, length)
    scale = 1.0 / queries.shape[-1] ** 0.5
    key_acc = jnp.zeros(keys.shape, jnp.float32)
    value_acc = jnp.zeros(values.shape, jnp.float32)
    query_parts = []
    for start in range(0, length, block_rows):
        rows = slice(start, start + block_rows)
        query_block = queries[rows]
        scores = block_scores(query_block, keys, positions[rows], positions)
        probs = jnp.exp(scores - totals[:, rows][..., None])
        grad_block = out_grad[rows]
        value_acc = value_acc + jnp.einsum(
            "hqk,qhd->khd",
            probs.astype(jnp.bfloat16),
            grad_block,
            preferred_element_type=jnp.float32,
        )
        prob_grad = jnp.einsum(
            "qhd,khd->hqk", grad_block, values, preferred_element_type=jnp.float32
        )
        delta = jnp.sum(
            grad_block.astype(jnp.float32) * outputs[rows].astype(jnp.float32),
            axis=-1,
        ).T
        score_grad = (probs * (prob_grad - delta[..., None])).astype(jnp.bfloat16)
        query_parts.append(
            (
                jnp.einsum("hqk,khd->qhd", score_grad, keys, preferred_element_type=jnp.float32)
                * scale
            ).astype(jnp.bfloat16)
        )
        key_acc = (
            key_acc
            + jnp.einsum(
                "hqk,qhd->khd", score_grad, query_block, preferred_element_type=jnp.float32
            )
            * scale
        )
    return (
        jnp.concatenate(query_parts, axis=0),
        key_acc.astype(jnp.bfloat16),
        value_acc.astype(jnp.bfloat16),
    )


def shift(array, axis_name, step):
    size = lax.axis_size(axis_name)
    return lax.ppermute(array, axis_name, [(i, (i + step) % size) for i in range(size)])


def around(array, axis_name, dim):
    size = lax.axis_size(axis_name)
    return jnp.concatenate(
        [array] + [shift(array, axis_name, step) for step in range(1, size)], axis=dim
    )


def group_rows(array):
    return around(around(array, "ctx", 1), "tensor", 1)


def sum_around(array, axis_name):
    size = lax.axis_size(axis_name)
    part = array.shape[1] // size
    total = array[:, :part].astype(jnp.float32)
    for step in range(1, size):
        piece = array[:, step * part : (step + 1) * part].astype(jnp.bfloat16)
        total = total + shift(piece, axis_name, -step).astype(jnp.float32)
    return total


def group_sum(array):
    return sum_around(sum_around(array, "tensor"), "ctx")


def in_order(array, axis_name, dim):
    size = lax.axis_size(axis_name)
    me = lax.axis_index(axis_name)
    width = array.shape[dim]
    shape = list(array.shape)
    shape[dim] = width * size
    out = jnp.zeros(shape, array.dtype)
    for step in range(size):
        piece = array if step == 0 else shift(array, axis_name, step)
        owner = lax.rem(me - step + size, size)
        out = lax.dynamic_update_slice_in_dim(out, piece, owner * width, dim)
    return out


def part_of(array, dim, count, start):
    return lax.dynamic_slice_in_dim(array, start, count, dim)


def shards(
    block_input,
    operator_gain,
    query_weight,
    key_weight,
    value_weight,
    output_weight,
    feedforward_gain,
    gate_weight,
    up_weight,
    down_weight,
    query_gain,
    key_gain,
    cotangent,
):
    bf16 = jnp.bfloat16
    f32 = jnp.float32
    fsdp = lax.axis_size("fsdp")
    ctx = lax.axis_size("ctx")
    tensor = lax.axis_size("tensor")
    me_f = lax.axis_index("fsdp")
    me_c = lax.axis_index("ctx")
    me_t = lax.axis_index("tensor")
    seqs, tok_here, width = block_input.shape
    quarter = tok_here // tensor
    tokens = tok_here * ctx
    rows = seqs * tokens
    gain_rows = query_gain.shape[0]
    head_width = gain_rows * fsdp
    heads_shard = query_weight.shape[1] // head_width
    kv_shard = key_weight.shape[1] // head_width
    spread = heads_shard // kv_shard
    heads = heads_shard // ctx
    kv = max(1, kv_shard // ctx)
    group = heads // kv
    copies = max(1, ctx // kv_shard)
    q_cols = heads * head_width
    kv_cols = kv * head_width
    kv_start = ((me_c * heads) // spread) * head_width
    hidden_units = gate_weight.shape[1] // ctx
    shard_rows = query_weight.shape[0]

    gains = jnp.stack(
        [
            operator_gain,
            feedforward_gain,
            jnp.pad(query_gain, (0, shard_rows - gain_rows)),
            jnp.pad(key_gain, (0, shard_rows - gain_rows)),
        ],
        axis=1,
    )
    attention_pack = jnp.concatenate(
        [
            part_of(query_weight, 1, q_cols, me_c * q_cols),
            part_of(key_weight, 1, kv_cols, kv_start),
            part_of(value_weight, 1, kv_cols, kv_start),
            part_of(output_weight, 0, q_cols, me_c * q_cols).T,
            jnp.pad(gains, ((0, 0), (0, 124))),
        ],
        axis=1,
    )
    feedforward_pack = jnp.concatenate(
        [
            part_of(gate_weight, 1, hidden_units, me_c * hidden_units),
            part_of(up_weight, 1, hidden_units, me_c * hidden_units),
            part_of(down_weight, 0, hidden_units, me_c * hidden_units).T,
        ],
        axis=1,
    )
    attention_full = lax.all_gather(attention_pack, "fsdp", axis=0, tiled=True)
    feedforward_full = lax.all_gather(feedforward_pack, "fsdp", axis=0, tiled=True)
    gate_up_full = feedforward_full[:, : 2 * hidden_units]
    down_full = feedforward_full[:, 2 * hidden_units :]
    qkv_cols = q_cols + 2 * kv_cols
    qkv_full = attention_full[:, :qkv_cols]
    output_full = attention_full[:, qkv_cols : qkv_cols + q_cols]
    gains_full = attention_full[:, qkv_cols + q_cols :].astype(f32)
    operator_scale = gains_full[:, 0]
    feedforward_scale = gains_full[:, 1]
    query_scale = gains_full[:, 2].reshape(fsdp, shard_rows)[:, :gain_rows].reshape(-1)
    key_scale = gains_full[:, 3].reshape(fsdp, shard_rows)[:, :gain_rows].reshape(-1)

    own_input = part_of(block_input, 1, quarter, me_t * quarter)
    all_input = group_rows(own_input).reshape(rows, width)
    upstream_own = part_of(cotangent, 1, quarter, me_t * quarter)
    upstream = group_rows(upstream_own).reshape(rows, width)

    ctx_order = lax.rem(me_c - jnp.arange(ctx) + ctx, ctx)
    tensor_order = lax.rem(me_t - jnp.arange(tensor) + tensor, tensor)
    positions = (
        tensor_order[:, None, None] * quarter
        + ctx_order[None, :, None] * tok_here
        + jnp.arange(quarter)[None, None, :]
    ).reshape(tokens)
    cosine, sine = rotary_tables(positions, head_width)

    def prepare(raw, gain):
        return head_prepare(raw, gain, cosine, sine)

    normed_input = rms_scale(all_input.astype(f32), operator_scale).astype(bf16)
    qkv_raw = jnp.dot(normed_input, qkv_full, preferred_element_type=f32).reshape(seqs, tokens, -1)
    query_f32, query_back = jax.vjp(prepare, qkv_raw[..., :q_cols], query_scale)
    key_f32, key_back = jax.vjp(prepare, qkv_raw[..., q_cols : q_cols + kv_cols], key_scale)
    queries = query_f32.astype(bf16)
    keys = jnp.repeat(key_f32.astype(bf16), group, axis=2)
    values = jnp.repeat(
        qkv_raw[..., q_cols + kv_cols :].astype(bf16).reshape(seqs, tokens, kv, head_width),
        group,
        axis=2,
    )
    attended, totals = jax.vmap(attend, in_axes=(0, 0, 0, None))(queries, keys, values, positions)
    attended_rows = attended.reshape(rows, q_cols)
    attention_part = contract(attended_rows, output_full, 1, 1).reshape(seqs, tokens, width)
    own_f32 = own_input.astype(f32)
    hidden = own_f32 + group_sum(attention_part)
    norm_two, norm_two_back = jax.vjp(rms_scale, hidden, feedforward_scale)
    normed_hidden = group_rows(norm_two.astype(bf16)).reshape(rows, width)
    gate_up = jnp.dot(normed_hidden, gate_up_full, preferred_element_type=f32)
    act_f32, act_back = jax.vjp(swiglu, gate_up[:, :hidden_units], gate_up[:, hidden_units:])
    activation = act_f32.astype(bf16)
    act_grad = jnp.dot(upstream, down_full, preferred_element_type=f32)
    gate_grad, up_grad = act_back(act_grad)
    gate_up_grad = jnp.concatenate([gate_grad.astype(bf16), up_grad.astype(bf16)], axis=1)
    hidden_part = contract(gate_up_grad, gate_up_full, 1, 1).reshape(seqs, tokens, width)
    feedforward_grad = jnp.concatenate(
        [
            contract(normed_hidden, gate_up_grad, 0, 0).astype(bf16),
            contract(upstream, activation, 0, 0).astype(bf16),
        ],
        axis=1,
    )
    normed_hidden_grad, feedforward_grad = lax.optimization_barrier(
        (group_sum(hidden_part), feedforward_grad)
    )
    feedforward_share = lax.psum_scatter(
        feedforward_grad, "fsdp", scatter_dimension=0, tiled=True
    )
    down_part = contract(activation, down_full, 1, 1).reshape(seqs, tokens, width)
    own_output = (hidden + group_sum(down_part)).astype(bf16)
    block_output = in_order(own_output, "tensor", 1)

    hidden_norm_grad, feedforward_gain_grad = norm_two_back(normed_hidden_grad)
    hidden_grad = upstream_own.astype(f32) + hidden_norm_grad
    hidden_grad_b = group_rows(hidden_grad.astype(bf16)).reshape(rows, width)
    output_weight_grad = contract(hidden_grad_b, attended_rows, 0, 0)
    attended_grad = (
        jnp.dot(hidden_grad_b, output_full, preferred_element_type=f32)
        .astype(bf16)
        .reshape(seqs, tokens, heads, head_width)
    )
    query_hgrad, key_hgrad, value_hgrad = jax.vmap(attend_grad, in_axes=(0, 0, 0, 0, 0, 0, None))(
        queries, keys, values, attended, totals, attended_grad, positions
    )

    def head_sum(grad):
        return grad.astype(f32).reshape(seqs, tokens, kv, group, head_width).sum(axis=3)

    query_pre, query_gain_grad = query_back(query_hgrad.astype(f32))
    key_pre, key_gain_grad = key_back(head_sum(key_hgrad))
    qkv_raw_grad = jnp.concatenate(
        [
            query_pre.astype(bf16).reshape(rows, q_cols),
            key_pre.astype(bf16).reshape(rows, kv_cols),
            head_sum(value_hgrad).astype(bf16).reshape(rows, kv_cols),
        ],
        axis=1,
    )
    input_part = contract(qkv_raw_grad, qkv_full, 1, 1).reshape(seqs, tokens, width)
    normed_input_grad = group_sum(input_part)
    qkv_weight_grad = contract(normed_input, qkv_raw_grad, 0, 0)
    attention_grad = jnp.concatenate([qkv_weight_grad, output_weight_grad], axis=1).astype(bf16)
    attention_grad, feedforward_share = lax.optimization_barrier(
        (attention_grad, feedforward_share)
    )
    attention_share = lax.psum_scatter(attention_grad, "fsdp", scatter_dimension=0, tiled=True)
    gate_up_share = feedforward_share[:, : 2 * hidden_units]
    down_share = feedforward_share[:, 2 * hidden_units :]
    _, norm_one_back = jax.vjp(rms_scale, own_f32, operator_scale)
    input_norm_grad, operator_gain_grad = norm_one_back(normed_input_grad)
    input_grad = in_order(hidden_grad + input_norm_grad, "tensor", 1)

    gain_sums = lax.psum(
        jnp.concatenate([operator_gain_grad, feedforward_gain_grad, query_gain_grad, key_gain_grad]),
        ("fsdp", "ctx", "tensor"),
    )
    operator_share = part_of(gain_sums, 0, shard_rows, me_f * shard_rows)
    feedforward_gain_share = part_of(gain_sums, 0, shard_rows, width + me_f * shard_rows)
    query_gain_share = part_of(gain_sums, 0, gain_rows, 2 * width + me_f * gain_rows)
    key_gain_share = part_of(gain_sums, 0, gain_rows, 2 * width + head_width + me_f * gain_rows)

    def spread_cols(share):
        return in_order(share, "ctx", 1).astype(f32)

    def spread_heads(share):
        if copies == 1:
            return spread_cols(share)
        every = in_order(share, "ctx", 1).astype(f32)
        return every.reshape(shard_rows, kv_shard, copies, head_width).sum(axis=2).reshape(
            shard_rows, -1
        )

    return (
        block_output,
        input_grad,
        operator_share,
        spread_cols(attention_share[:, :q_cols]),
        spread_heads(attention_share[:, q_cols : q_cols + kv_cols]),
        spread_heads(attention_share[:, q_cols + kv_cols : qkv_cols]),
        in_order(attention_share[:, qkv_cols:].T, "ctx", 0).astype(f32),
        feedforward_gain_share,
        spread_cols(gate_up_share[:, :hidden_units]),
        spread_cols(gate_up_share[:, hidden_units:]),
        in_order(down_share.T, "ctx", 0).astype(f32),
        query_gain_share,
        key_gain_share,
    )


def solution(mesh):
    in_specs = (
        P("fsdp", "ctx", None),
        P("fsdp"),
        P("fsdp", "tensor"),
        P("fsdp", "tensor"),
        P("fsdp", "tensor"),
        P("tensor", "fsdp"),
        P("fsdp"),
        P("fsdp", "tensor"),
        P("fsdp", "tensor"),
        P("tensor", "fsdp"),
        P("fsdp"),
        P("fsdp"),
        P("fsdp", "ctx", None),
    )
    out_specs = (
        P("fsdp", "ctx", None),
        P("fsdp", "ctx", None),
        P("fsdp"),
        P("fsdp", "tensor"),
        P("fsdp", "tensor"),
        P("fsdp", "tensor"),
        P("tensor", "fsdp"),
        P("fsdp"),
        P("fsdp", "tensor"),
        P("fsdp", "tensor"),
        P("tensor", "fsdp"),
        P("fsdp"),
        P("fsdp"),
    )
    return jax.shard_map(shards, mesh=mesh, in_specs=in_specs, out_specs=out_specs, check_vma=False)
```
